32 devices in a mesh: fsdp: 2 (over core), context: 4 (over y, x), tensor: 4 (over z).
Axes of the slice: x: 2, y: 2, z: 4, core: 2. Of those that a mesh axis runs over, the one named last changes fastest.
Arguments:
- hidden: bfloat16 [8192, 1536], P(('fsdp', 'context')), may hold values from -6 to 6
- norm_gain: bfloat16 [1536], P('fsdp'), may hold values from 0.5 to 1.5
- w_gate: bfloat16 [1536, 3072], P('fsdp', 'tensor'), may hold values from -0.15625 to 0.15625
- w_input: bfloat16 [1536, 3072], P('fsdp', 'tensor'), may hold values from -0.15625 to 0.15625
- w_bc: bfloat16 [1536, 256], P('fsdp', 'tensor'), may hold values from -0.15625 to 0.15625
- w_dt: bfloat16 [1536, 48], P('fsdp', 'tensor'), may hold values from -0.15625 to 0.15625
- conv_x: bfloat16 [4, 3072], P(None, ('tensor', 'fsdp')), may hold values from -2 to 2
- conv_bc: bfloat16 [4, 256], P(None, ('tensor', 'fsdp')), may hold values from -2 to 2
- bias_x: bfloat16 [3072], P(('tensor', 'fsdp')), may hold values from -0.5 to 0.5
- bias_bc: bfloat16 [256], P(('tensor', 'fsdp')), may hold values from -0.5 to 0.5
- dt_bias: bfloat16 [48], P(('tensor', 'fsdp')), may hold values from -6 to -2
- a_log: bfloat16 [48], P(('tensor', 'fsdp')), may hold values from -2 to 1.5
- skip_d: bfloat16 [48], P(('tensor', 'fsdp')), may hold values from 0.5 to 1.5
- out_gain: bfloat16 [3072], P(('tensor', 'fsdp')), may hold values from 0.5 to 1.5
- w_out: bfloat16 [3072, 1536], P('tensor', 'fsdp'), may hold values from -0.109375 to 0.109375
- cotangent: bfloat16 [8192, 1536], P(('fsdp', 'context')), may hold values from -6 to 6
- doc_start: int32 [8192], P(('fsdp', 'context')), may hold values from 0 to 1, as said below
- valid: int32 [8192], P(('fsdp', 'context')), may hold values 0 or 1
Outputs:
- mixed: bfloat16 [8192, 1536], P(('fsdp', 'context'))
- grad_hidden: float32 [8192, 1536], P(('fsdp', 'context'))
- grad_norm_gain: float32 [1536], P('fsdp')
- grad_w_gate: float32 [1536, 3072], P('fsdp', 'tensor')
- grad_w_input: float32 [1536, 3072], P('fsdp', 'tensor')
- grad_w_bc: float32 [1536, 256], P('fsdp', 'tensor')
- grad_w_dt: float32 [1536, 48], P('fsdp', 'tensor')
- grad_conv_x: float32 [4, 3072], P(None, ('tensor', 'fsdp'))
- grad_conv_bc: float32 [4, 256], P(None, ('tensor', 'fsdp'))
- grad_bias_x: float32 [3072], P(('tensor', 'fsdp'))
- grad_bias_bc: float32 [256], P(('tensor', 'fsdp'))
- grad_dt_bias: float32 [48], P(('tensor', 'fsdp'))
- grad_a_log: float32 [48], P(('tensor', 'fsdp'))
- grad_skip_d: float32 [48], P(('tensor', 'fsdp'))
- grad_out_gain: float32 [3072], P(('tensor', 'fsdp'))
- grad_w_out: float32 [3072, 1536], P('tensor', 'fsdp')
The draws below stay inside these ranges and needn't reach their ends.
Inputs may be any that keep to these rules, and one draw needn't show every extreme that they name: doc_start is 1 at the first token of every group of 4096 tokens and at the first token of every later document of the group; every document that ends inside its group has 1024 to 4096 tokens.
All inputs are finite; a program needn't handle non-finite values. No bound on the sum of `valid` on one device may be relied on, other than what follows from the above.
Results may differ from the reference program's by a relative error of at most 0.02.
Values may be sent and summed in bfloat16 or wider, within the bound.
No kernel may reach another device: no remote copies, remote signals or barrier semaphores. Data moves between devices by JAX's collectives and lax.ppermute only.
A program may use at most 192 MiB of HBM per device.

```python
import jax
import jax.numpy as jnp
from jax import lax

D = 1536
HEADS = 48
HEAD_DIM = 64
STATE = 128
WIDTH = 4
BLOCK = 256
SEQ_MIN = 1024
INNER = 3072
GROUP = 4096
TOKENS = 8192
N_FSDP = 2


def draw_doc_start(key, part):
    groups = TOKENS // GROUP
    doc_count = GROUP // SEQ_MIN + 1
    lengths = jax.random.randint(key, (groups, doc_count), SEQ_MIN, 4 * SEQ_MIN + 1)
    doc_ends = jnp.cumsum(lengths, axis=1)
    position = jnp.arange(GROUP)
    boundary = jnp.any(position[None, :, None] == doc_ends[:, None, :], axis=2) | (position[None, :] == 0)
    return boundary.astype(jnp.int32).reshape(TOKENS)


def touch_ends(entries, stream_key, low, top_value):
    place = [jax.random.randint(jax.random.fold_in(stream_key, axis), (), 0, length) for axis, length in enumerate(entries.shape)]
    main_axis = entries.shape.index(max(entries.shape))
    beside = place[:main_axis] + [(place[main_axis] + 1) % entries.shape[main_axis]] + place[main_axis + 1:]
    return entries.at[tuple(place)].set(low).at[tuple(beside)].set(top_value)


def shard_levels(stream_key, dims, cuts, smallest, high):
    gain = 1.0
    for dim, shards_of in cuts:
        steps = jax.random.uniform(jax.random.fold_in(jax.random.fold_in(stream_key, 6), dim), (shards_of,), jnp.float32, smallest / len(cuts), high / len(cuts))
        gain = gain * jnp.repeat(jnp.exp(steps), dims[dim] // shards_of).reshape((-1,) + (1,) * (len(dims) - 1 - dim))
    return gain


def noise(own_key, dims, deviation, limit, shards=(), kind=jnp.bfloat16):
    values = jax.random.normal(own_key, dims, jnp.float32) * deviation
    if len(shards) > 0:
        values = shard_levels(own_key, dims, shards, -0.22, 0.18) * values
    return jnp.clip(values, min=-limit, max=limit).astype(kind)


def setup_inputs(seed: int = 0) -> dict:
    streams_of = jax.random.split(jax.random.key(seed), 19)
    return {
        "hidden": noise(streams_of[0], (TOKENS, D), 1.0, 6.0, ((0, 8),)),
        "norm_gain": jnp.clip(1.0 + 0.1 * jax.random.normal(streams_of[1], (D,), jnp.float32), 0.5, 1.5).astype(jnp.bfloat16),
        "w_gate": noise(streams_of[2], (D, INNER), D ** -0.5, 0.15625, ((0, 2), (1, 4))),
        "w_input": noise(streams_of[3], (D, INNER), D ** -0.5, 0.15625, ((0, 2), (1, 4))),
        "w_bc": noise(streams_of[4], (D, 2 * STATE), D ** -0.5, 0.15625, ((0, 2), (1, 4))),
        "w_dt": noise(streams_of[5], (D, HEADS), D ** -0.5, 0.15625, ((0, 2), (1, 4))),
        "conv_x": noise(streams_of[6], (WIDTH, INNER), 0.5, 2.0, ((1, 8),)),
        "conv_bc": noise(streams_of[7], (WIDTH, 2 * STATE), 0.5, 2.0, ((1, 8),)),
        "bias_x": jnp.clip(jax.random.uniform(streams_of[8], (INNER,), jnp.float32, -0.5, 0.5) * shard_levels(streams_of[8], (INNER,), ((0, 8),), -0.4, 0.0), -0.5, 0.5).astype(jnp.bfloat16),
        "bias_bc": jnp.clip(jax.random.uniform(streams_of[9], (2 * STATE,), jnp.float32, -0.5, 0.5) * shard_levels(streams_of[9], (2 * STATE,), ((0, 8),), -0.4, 0.0), -0.5, 0.5).astype(jnp.bfloat16),
        "dt_bias": jnp.clip(-6.0 + 4.0 * jax.random.uniform(streams_of[10], (HEADS,), jnp.float32) ** shard_levels(streams_of[10], (HEADS,), ((0, 8),), -0.2, 0.2), -6.0, -2.0).astype(jnp.bfloat16),
        "a_log": jnp.clip(-2.0 + 3.5 * jax.random.uniform(streams_of[11], (HEADS,), jnp.float32) ** shard_levels(streams_of[11], (HEADS,), ((0, 8),), -0.2, 0.2), -2.0, 1.5).astype(jnp.bfloat16),
        "skip_d": jnp.clip(0.5 + 1.0 * jax.random.uniform(streams_of[12], (HEADS,), jnp.float32) ** shard_levels(streams_of[12], (HEADS,), ((0, 8),), -0.2, 0.2), 0.5, 1.5).astype(jnp.bfloat16),
        "out_gain": jnp.clip(1.0 + 0.1 * jax.random.normal(streams_of[13], (INNER,), jnp.float32), 0.5, 1.5).astype(jnp.bfloat16),
        "w_out": noise(streams_of[14], (INNER, D), INNER ** -0.5, 0.109375, ((0, 4), (1, 2))),
        "cotangent": noise(streams_of[15], (TOKENS, D), 1.0, 6.0, ((0, 8),)),
        "doc_start": draw_doc_start(jax.random.fold_in(streams_of[18], 71), 0),
        "valid": touch_ends((jax.random.randint(streams_of[17], (TOKENS,), 0, 8) < 7).astype(jnp.int32), jax.random.fold_in(streams_of[17], 1), 0, 1),
    }


exact_mode = lax.Precision.HIGHEST
epsilon = 1e-05

@jax.custom_vjp
def low(v):
    return lax.optimization_barrier(v.astype(jnp.bfloat16)).astype(jnp.float32)

@jax.custom_vjp
def low_back(v):
    return v

def low_keep(v):
    return (low(v), None)

def low_pass(kept, grad):
    return (grad,)

def back_keep(v):
    return (v, None)

def back_low(kept, grad):
    return (low(grad),)
low.defvjp(low_keep, low_pass)
low_back.defvjp(back_keep, back_low)

def matmul(first_operand, second_operand):
    return jnp.dot(first_operand, second_operand, precision=exact_mode, preferred_element_type=jnp.float32)

def causal_conv(conv_input, kernel, offsets, group_counts):
    channels = conv_input.shape[1]
    grouped = conv_input.reshape(N_FSDP, GROUP, channels)
    padded = jnp.pad(grouped, ((0, 0), (WIDTH - 1, 0), (0, 0)))
    padded_counts = jnp.pad(group_counts, ((0, 0), (WIDTH - 1, 0)))
    running = jnp.zeros(grouped.shape, jnp.float32) + offsets[None, None, :]
    for offset in range(WIDTH):
        doc_mask = (group_counts == padded_counts[:, offset:offset + GROUP]).astype(jnp.float32)
        running = running + kernel[offset][None, None, :] * padded[:, offset:offset + GROUP] * doc_mask[..., None]
    return running.reshape(-1, channels)

def block_step(skip_gain, state_prior, pieces):
    inner_block, write_block, read_block, step_block, log_block, count_block = pieces
    log_cum = jnp.cumsum(log_block, axis=1)
    position = jnp.arange(BLOCK)
    lower = (position[:, None] >= position[None, :])[None]
    same_doc = lower & (count_block[:, :, None] == count_block[:, None, :])
    carry_live = (count_block == 0).astype(jnp.float32)
    cum_heads = jnp.swapaxes(log_cum, 1, 2)
    spread = cum_heads[:, :, :, None] - cum_heads[:, :, None, :]
    same_heads = same_doc[:, None]
    decay_mask = jnp.where(same_heads, jnp.exp(jnp.where(same_heads, spread, 0.0)), 0.0)
    weights_mix = decay_mask * jnp.swapaxes(step_block, 1, 2)[:, :, None, :]
    scores = low_back(jnp.einsum('gtn,gsn->gts', read_block, write_block, precision=exact_mode))
    mixing = low(scores[:, None] * weights_mix)
    intra = jnp.einsum('ghts,gshp->gthp', mixing, inner_block, precision=exact_mode)
    read_gain = jnp.exp(log_cum) * carry_live[..., None]
    prior_low = low(state_prior)
    carried = low_back(jnp.einsum('gtn,ghpn->gthp', read_block, prior_low, precision=exact_mode))
    output = low_back(intra + read_gain[..., None] * carried + skip_gain[None, None, :, None] * inner_block)
    end_weight = same_doc[:, -1, :].astype(jnp.float32)
    write_gain = jnp.exp(log_cum[:, -1:, :] - log_cum) * end_weight[..., None] * step_block
    scaled = low(inner_block * write_gain[..., None])
    state_add = low_back(jnp.einsum('glhp,gln->ghpn', scaled, write_block, precision=exact_mode))
    block_decay = jnp.exp(log_cum[:, -1, :]) * carry_live[:, -1, None]
    return (block_decay[..., None, None] * state_prior + state_add, output)

def reference(hidden, norm_gain, w_gate, w_input, w_bc, w_dt, conv_x, conv_bc, bias_x, bias_bc, dt_bias, a_log, skip_d, out_gain, w_out, cotangent, doc_start, valid):
    group_counts = jnp.cumsum(doc_start.reshape(N_FSDP, GROUP), axis=1, dtype=jnp.int32)
    block_counts = jnp.cumsum(doc_start.reshape(N_FSDP, GROUP // BLOCK, BLOCK), axis=2, dtype=jnp.int32)
    block_counts = jnp.moveaxis(block_counts, 1, 0)
    valid_float = valid.astype(jnp.float32)
    stepper = jax.checkpoint(block_step)

    def to_blocks(values):
        shaped = values.reshape((N_FSDP, GROUP // BLOCK, BLOCK) + values.shape[1:])
        return jnp.moveaxis(shaped, 1, 0)

    def forward(hidden, norm_gain, w_gate, w_input, w_bc, w_dt, conv_x, conv_bc, bias_x, bias_bc, dt_bias, a_log, skip_d, out_gain, w_out):
        inverse_rms = lax.rsqrt(lax.optimization_barrier(jnp.mean(hidden * hidden, axis=1, keepdims=True)) + epsilon)
        normed = low(hidden * inverse_rms * norm_gain[None, :])
        gate_pre = low_back(matmul(normed, w_gate))
        step_raw = low_back(matmul(normed, w_dt))
        inner_in = low_back(low(matmul(normed, w_input)))
        state_in = low_back(low(matmul(normed, w_bc)))
        pre_inner = causal_conv(inner_in, conv_x, bias_x, group_counts)
        pre_state = causal_conv(state_in, conv_bc, bias_bc, group_counts)
        inner_act = low(jax.nn.silu(pre_inner))
        state_act = low(jax.nn.silu(pre_state))
        step_size = jax.nn.softplus(step_raw + dt_bias[None, :]) * valid_float[:, None]
        decay_rate = -jnp.exp(a_log)
        log_step = step_size * decay_rate[None, :]
        pieces = (to_blocks(inner_act.reshape(-1, HEADS, HEAD_DIM)), to_blocks(state_act[:, :STATE]), to_blocks(state_act[:, STATE:]), to_blocks(step_size), to_blocks(log_step), block_counts)
        start_state = jnp.zeros((N_FSDP, HEADS, HEAD_DIM, STATE), jnp.float32)
        final_state, outputs = lax.scan(lambda state_prior, block_pieces: stepper(skip_d, state_prior, block_pieces), start_state, pieces)
        ssd_out = jnp.moveaxis(outputs, 0, 1).reshape(-1, INNER)
        gated = ssd_out * jax.nn.silu(gate_pre)
        inverse_gate = lax.rsqrt(lax.optimization_barrier(jnp.mean(gated * gated, axis=1, keepdims=True)) + epsilon)
        normed_out = low(gated * inverse_gate * out_gain[None, :])
        return hidden + matmul(normed_out, w_out)
    floats = (hidden, norm_gain, w_gate, w_input, w_bc, w_dt, conv_x, conv_bc, bias_x, bias_bc, dt_bias, a_log, skip_d, out_gain, w_out)
    floats = tuple((entry.astype(jnp.float32) for entry in floats))
    mixed, pullback = jax.vjp(forward, *floats)
    grads = pullback(cotangent.astype(jnp.float32))
    return (mixed.astype(jnp.bfloat16), grads[0], grads[1], grads[2], grads[3], grads[4], grads[5], grads[6], grads[7], grads[8], grads[9], grads[10], grads[11], grads[12], grads[13], grads[14])
```

```python
import functools

import jax
import jax.numpy as jnp
from jax import lax
from jax.experimental import pallas as pl
from jax.experimental.pallas import tpu as pltpu
from jax.sharding import PartitionSpec as P

HEAD_DIM = 64
STATE = 128
WIDTH = 4
BLOCK = 256
EPSILON = 1e-05
LANES = 128
PAY = STATE + 16


F32 = jnp.float32
BF16 = jnp.bfloat16
NN = ((1,), (0,))
NT = ((1,), (1,))
TN = ((0,), (0,))
EXACT = lax.Precision.HIGHEST


def mm(a, b, dims=NN, precision=None):
    return lax.dot_general(
        a, b, (dims, ((), ())), precision=precision, preferred_element_type=F32
    )


def iota(shape, axis):
    return lax.broadcasted_iota(jnp.int32, shape, axis)


def split(x):
    high = x.astype(BF16)
    return high, (x - high.astype(F32)).astype(BF16)


def head_map(channels):
    shape = (LANES, channels)
    return (iota(shape, 1) // HEAD_DIM == iota(shape, 0)).astype(BF16)


def expand(x, spread):
    high, low = split(x)
    return mm(high, spread) + mm(low, spread)


def per_head(x, spread):
    high, low = split(x)
    return mm(high, spread, NT) + mm(low, spread, NT)


def sigmoid(x):
    return 1.0 / (1.0 + jnp.exp(-x))


def softplus(x):
    return jnp.maximum(x, 0.0) + jnp.log1p(jnp.exp(-jnp.abs(x)))


def silu_slope(x):
    s = sigmoid(x)
    return s * (1.0 + x * (1.0 - s))


def incoming(refs):
    total = None
    for ref in reversed(refs):
        state = ref[0:STATE, :].astype(F32)
        if total is None:
            total = state
        else:
            total = state + ref[STATE : STATE + 1, :].astype(F32) * total
    return total


def counts_of(rows):
    at = (iota((BLOCK, BLOCK), 1) <= iota((BLOCK, BLOCK), 0)).astype(BF16)
    column = mm(at, rows, NT)[:, 0:1]
    row = mm(rows, at, NT)[0:1, :]
    return column, row


def columns_of(rows):
    eye = (iota((BLOCK, BLOCK), 1) == iota((BLOCK, BLOCK), 0)).astype(BF16)
    return mm(eye, rows, NT)


def k_do(f_ref, ct_ref, own_w, oth_w, do_ref, own_ref, oth_ref):
    half = own_ref.shape[1]

    @pl.when(f_ref[0] == 0)
    def _():
        own_ref[...] = ct_ref[:, :half]
        oth_ref[...] = ct_ref[:, half:]

    @pl.when(f_ref[0] != 0)
    def _():
        own_ref[...] = ct_ref[:, half:]
        oth_ref[...] = ct_ref[:, :half]

    do_ref[...] = (
        mm(own_ref[...], own_w[...], NT) + mm(oth_ref[...], oth_w[...], NT)
    ).astype(BF16)


def k_project(f_ref, h_ref, gain_ref, wi_own, wi_oth, ws_own, ws_oth, own_ref, oth_ref, x_ref, dt_ref):
    half = own_ref.shape[1]
    inner = wi_own.shape[1]
    res = h_ref[...].astype(F32)
    scale = lax.rsqrt(jnp.mean(res * res, axis=1, keepdims=True) + EPSILON)
    normed = (res * scale * gain_ref[...]).astype(BF16)

    @pl.when(f_ref[0] == 0)
    def _():
        own_ref[...] = normed[:, :half]
        oth_ref[...] = normed[:, half:]

    @pl.when(f_ref[0] != 0)
    def _():
        own_ref[...] = normed[:, half:]
        oth_ref[...] = normed[:, :half]

    own, oth = own_ref[...], oth_ref[...]
    x_ref[:, :inner] = (mm(own, wi_own[...]) + mm(oth, wi_oth[...])).astype(BF16)
    small = mm(own, ws_own[0:half, :]) + mm(oth, ws_oth[0:half, :])
    x_ref[:, inner:] = small[:, : 2 * STATE].astype(BF16)
    dt_ref[...] = small[:, 2 * STATE :]


def k_gate_in(own_ref, oth_ref, w_own, w_oth, z_ref):
    z_ref[...] = mm(own_ref[...], w_own[...]) + mm(oth_ref[...], w_oth[...])


def k_conv(
    rows_ref, x_ref, halo_ref, dtr_ref, hp_ref, cw_ref,
    act_ref, pre_ref, cs_ref, dt_ref, hl_ref, dc_ref, pay_ref,
    ext, state, decay,
):
    inner = state.shape[1]
    block = pl.program_id(0)

    @pl.when(block == 0)
    def _():
        ext[0:8, :] = halo_ref[...].astype(F32)
        state[...] = jnp.zeros_like(state)
        decay[...] = jnp.ones_like(decay)

    rows = rows_ref[...]
    cols = columns_of(rows)
    count, _ = counts_of(rows)
    x = x_ref[...].astype(F32)
    ext[8 : 8 + BLOCK, :] = x
    pre = cw_ref[4:5, :] + cw_ref[3:4, :] * x
    for back in range(1, WIDTH):
        pre = pre + cw_ref[3 - back : 4 - back, :] * ext[8 - back : 8 - back + BLOCK, :] * cols[
            :, 1 + back : 2 + back
        ]
    ext[0:8, :] = x[BLOCK - 8 :, :]
    pre_ref[...] = pre.astype(BF16)
    act = (pre * sigmoid(pre)).astype(BF16)
    act_ref[...] = act
    dt = softplus(dtr_ref[...] + hp_ref[0:1, :]) * cols[:, 1:2]
    lower = (iota((BLOCK, BLOCK), 1) <= iota((BLOCK, BLOCK), 0)).astype(F32)
    cs = mm(lower, dt * hp_ref[1:2, :], NN, EXACT)
    cs_ref[...] = cs
    dt_ref[...] = dt
    last = cs[BLOCK - 1 :, :]
    same = (count == count[BLOCK - 1 :, :]).astype(F32)
    spread = head_map(inner)
    write = expand(jnp.exp(last - cs) * dt * same, spread)
    scaled = (act[:, :inner].astype(F32) * write).astype(BF16)
    added = mm(act[:, inner : inner + STATE], scaled, TN)
    alive = (count[BLOCK - 1 :, :] < 0.5).astype(F32)
    step = expand(jnp.broadcast_to(jnp.exp(last) * alive, (8, LANES)), spread)
    hl_ref[...] = state[...]
    dc_ref[...] = decay[...]
    state[...] = step[0:1, :] * state[...] + added
    decay[...] = decay[...] * step

    @pl.when(block == pl.num_programs(0) - 1)
    def _():
        pay_ref[0:STATE, :] = state[...].astype(BF16)
        pay_ref[STATE:PAY, :] = jnp.concatenate([decay[...], decay[...]], axis=0).astype(BF16)


def k_heads(heads, rows_ref, act_ref, cs_ref, dt_ref, gf_ref, y_ref):
    inner = y_ref.shape[1]
    ccol, crow = counts_of(rows_ref[...])
    mask = (iota((BLOCK, BLOCK), 1) <= iota((BLOCK, BLOCK), 0)) & (ccol == crow)
    scores = mm(act_ref[:, inner + STATE :], act_ref[:, inner : inner + STATE], NT)
    cs = cs_ref[...]
    cs_t = jnp.transpose(cs)
    dt_t = jnp.transpose(dt_ref[...])
    low = iota((BLOCK, LANES), 1) < HEAD_DIM
    for pair in range(heads // 2):
        at = slice(pair * LANES, (pair + 1) * LANES)
        xs = act_ref[:, at]
        parts = []
        for h in (2 * pair, 2 * pair + 1):
            gap = jnp.where(mask, cs[:, h : h + 1] - cs_t[h : h + 1, :], -1e30)
            mix = (scores * (jnp.exp(gap) * dt_t[h : h + 1, :])).astype(BF16)
            parts.append(mm(mix, xs))
        y_ref[:, at] = jnp.where(low, parts[0], parts[1]) + gf_ref[1:2, at] * xs.astype(F32)


def k_gate(n_pay, rows_ref, act_ref, cs_ref, y0_ref, hl_ref, dc_ref, z_ref, do_ref, gf_ref, *rest):
    pays, (y_ref, o_ref, st_ref) = rest[:n_pay], rest[n_pay:]
    inner = y_ref.shape[1]
    count, _ = counts_of(rows_ref[...])
    state = hl_ref[...] + dc_ref[0:1, :] * incoming(pays)
    carried = mm(act_ref[:, inner + STATE :], state.astype(BF16))
    read = expand(jnp.exp(cs_ref[...]) * (count < 0.5).astype(F32), head_map(inner))
    y = y0_ref[...] + read * carried
    y_ref[...] = y
    z = z_ref[...]
    gated = y * (z * sigmoid(z))
    weighted = gated * gf_ref[0:1, :]
    o_ref[...] = weighted.astype(BF16)
    squares = jnp.sum(gated * gated, axis=1, keepdims=True)
    inner_product = jnp.sum(weighted * do_ref[...].astype(F32), axis=1, keepdims=True)
    lane = iota((BLOCK, LANES), 1)
    both = jnp.where(lane == 0, squares, jnp.where(lane == 1, inner_product, 0.0))
    st_ref[...] = jnp.transpose(both)[0:8, :]


def k_branch(f_ref, o_ref, w_own, w_oth, out_ref):
    half = w_own.shape[1]
    o = o_ref[...]
    own = mm(o, w_own[...]).astype(BF16)
    oth = mm(o, w_oth[...]).astype(BF16)

    @pl.when(f_ref[0] == 0)
    def _():
        out_ref[:, :half] = own
        out_ref[:, half:] = oth

    @pl.when(f_ref[0] != 0)
    def _():
        out_ref[:, :half] = oth
        out_ref[:, half:] = own


def k_back(
    heads, width, n_pay, rows_ref, act_ref, cs_ref, dt_ref, y_ref, z_ref, do_ref, hl_ref, dc_ref, gf_ref, st_ref, *rest
):
    pays = rest[:n_pay]
    dz_ref, o_ref, dxs_ref, dbc_ref, dcs_ref, w_ref, gl_ref, ec_ref, pay_ref, acc_ref = rest[n_pay : n_pay + 10]
    dxi, grad, decay = rest[n_pay + 10 :]
    inner = y_ref.shape[1]
    turn = pl.program_id(0)

    @pl.when(turn == 0)
    def _():
        grad[...] = jnp.zeros_like(grad)
        decay[...] = jnp.ones_like(decay)
        acc_ref[...] = jnp.zeros_like(acc_ref)

    stats = jnp.concatenate([st_ref[...], jnp.zeros((LANES - 8, BLOCK), F32)], axis=0)
    stats = jnp.transpose(stats)
    r2 = lax.rsqrt(stats[:, 0:1] / width + EPSILON)
    y, z = y_ref[...], z_ref[...]
    do = do_ref[...].astype(F32)
    gain = gf_ref[0:1, :]
    skip = gf_ref[1:2, :]
    sig = sigmoid(z)
    gate = z * sig
    gated = y * gate
    scaled = gated * r2
    o_ref[...] = (scaled * gain).astype(BF16)
    dgz = r2 * (do * gain) - gated * (r2 * r2 * r2 / width * stats[:, 1:2])
    dz_ref[...] = (dgz * y * (sig * (1.0 + z * (1.0 - sig)))).astype(BF16)
    dy = (dgz * gate).astype(BF16)
    dyf = dy.astype(F32)
    xs = act_ref[:, :inner]
    xsf = xs.astype(F32)
    acc_ref[0:1, :] += jnp.sum(do * scaled, axis=0, keepdims=True)
    acc_ref[1:2, :] += jnp.sum(dyf * xsf, axis=0, keepdims=True)

    ccol, crow = counts_of(rows_ref[...])
    mask = (iota((BLOCK, BLOCK), 0) <= iota((BLOCK, BLOCK), 1)) & (ccol == crow)
    bmat, cmat = act_ref[:, inner : inner + STATE], act_ref[:, inner + STATE :]
    scores = mm(bmat, cmat, NT)
    cs = cs_ref[...]
    cs_t = jnp.transpose(cs)
    dt = dt_ref[...]
    low = iota((BLOCK, LANES), 1) < HEAD_DIM
    dscore = jnp.zeros((BLOCK, BLOCK), F32)
    for pair in range(heads // 2):
        at = slice(pair * LANES, (pair + 1) * LANES)
        xp, dyp, dypf = xs[:, at], dy[:, at], dyf[:, at]
        parts = []
        for h in (2 * pair, 2 * pair + 1):
            gap = jnp.where(mask, cs_t[h : h + 1, :] - cs[:, h : h + 1], -1e30)
            weight = jnp.exp(gap) * dt[:, h : h + 1]
            parts.append(mm((scores * weight).astype(BF16), dyp))
            one = jnp.where(low if h % 2 == 0 else ~low, dypf, 0.0).astype(BF16)
            dscore = dscore + mm(xp, one, NT) * weight
        dxi[:, at] = jnp.where(low, parts[0], parts[1])
    dsb = dscore.astype(BF16)
    spread = head_map(inner)
    read = expand(jnp.exp(cs) * (ccol < 0.5).astype(F32), spread)
    dv = (dyf * read).astype(BF16)
    state = (hl_ref[...] + dc_ref[0:1, :] * incoming(pays)).astype(BF16)
    dbc_ref[:, :STATE] = mm(dsb, cmat)
    dbc_ref[:, STATE:] = mm(dsb, bmat, TN) + mm(dv, state, NT)
    entering = mm(cmat, dv, TN)
    w = per_head(xsf * dxi[...], spread)
    w_ref[...] = w
    dcs_ref[...] = per_head(dyf * (y - skip * xsf), spread) - w
    dxs_ref[...] = dxi[...] + skip * dyf
    alive = (ccol[BLOCK - 1 :, :] < 0.5).astype(F32)
    step = expand(jnp.broadcast_to(jnp.exp(cs[BLOCK - 1 :, :]) * alive, (8, LANES)), spread)
    gl_ref[...] = grad[...]
    ec_ref[...] = decay[...]
    grad[...] = entering + step[0:1, :] * grad[...]
    decay[...] = decay[...] * step

    @pl.when(turn == pl.num_programs(0) - 1)
    def _():
        pay_ref[0:STATE, :] = grad[...].astype(BF16)
        pay_ref[STATE:PAY, :] = jnp.concatenate([decay[...], decay[...]], axis=0).astype(BF16)


def k_back_state(
    n_pay, n_grad, rows_ref, act_ref, pre_ref, x_ref, halo_ref, cs_ref, dt_ref, dtr_ref, dxs_ref, dbc_ref, dcs_ref,
    w_ref, gl_ref, ec_ref, hl_ref, dc_ref, hp_ref, cw_ref, *rest
):
    pays = rest[:n_pay]
    grads = rest[n_pay : n_pay + n_grad]
    rest = rest[n_pay + n_grad :]
    din_ref, ddt_ref, edge_ref, cacc_ref, hacc_ref, ext1, ext2, ext3 = rest
    inner = dxs_ref.shape[1]
    channels = x_ref.shape[1]
    turn = pl.program_id(0)
    exts = (None, ext1, ext2, ext3)

    @pl.when(turn == 0)
    def _():
        cacc_ref[...] = jnp.zeros_like(cacc_ref)
        hacc_ref[...] = jnp.zeros_like(hacc_ref)
        for ext in exts[1:]:
            ext[8 + BLOCK :, :] = jnp.zeros((8, channels), F32)

    rows = rows_ref[...]
    cols = columns_of(rows)
    count, _ = counts_of(rows)
    spread = head_map(inner)
    cs, dt = cs_ref[...], dt_ref[...]
    last = cs[BLOCK - 1 :, :]
    same = (count == count[BLOCK - 1 :, :]).astype(F32)
    alive = (count[BLOCK - 1 :, :] < 0.5).astype(F32)
    write = expand(jnp.exp(last - cs) * dt * same, spread)
    leaving = gl_ref[...] + ec_ref[0:1, :] * incoming(grads)
    leaving_low = leaving.astype(BF16)
    state = hl_ref[...] + dc_ref[0:1, :] * incoming(pays)
    xsf = act_ref[:, :inner].astype(F32)
    through = mm(act_ref[:, inner : inner + STATE], leaving_low) * write
    dxs = dxs_ref[...] + through
    dbc = dbc_ref[...]
    dwrite = dbc[:, :STATE] + mm((xsf * write).astype(BF16), leaving_low, NT)
    w_end = per_head(xsf * through, spread)
    dot_state = per_head(
        jnp.broadcast_to(jnp.sum(leaving * state, axis=0, keepdims=True), (8, inner)), spread
    )[0:1, :]
    extra = jnp.sum(w_end, axis=0, keepdims=True) + jnp.exp(last) * alive * dot_state
    dcs = dcs_ref[...] - w_end
    dcs = dcs + jnp.where(iota((BLOCK, LANES), 0) == BLOCK - 1, extra, 0.0)
    upper = (iota((BLOCK, BLOCK), 1) >= iota((BLOCK, BLOCK), 0)).astype(F32)
    dla = mm(upper, dcs, NN, EXACT)
    valid = cols[:, 1:2]
    ratio = jnp.where(dt > 0.0, (w_ref[...] + w_end) / jnp.where(dt > 0.0, dt, 1.0), 0.0)
    dpre_dt = sigmoid(dtr_ref[...] + hp_ref[0:1, :]) * (ratio + dla * hp_ref[1:2, :] * valid)
    ddt_ref[...] = dpre_dt.astype(BF16)
    hacc_ref[0:1, :] += jnp.sum(dpre_dt, axis=0, keepdims=True)
    hacc_ref[1:2, :] += jnp.sum(dla * dt, axis=0, keepdims=True) * hp_ref[1:2, :]

    dact = jnp.concatenate([dxs, dwrite, dbc[:, STATE:]], axis=1)
    dpre = dact * silu_slope(pre_ref[...].astype(F32))
    x = x_ref[...].astype(F32)
    din = cw_ref[3:4, :] * dpre
    cacc_ref[3:4, :] += jnp.sum(x * dpre, axis=0, keepdims=True)
    cacc_ref[4:5, :] += jnp.sum(dpre, axis=0, keepdims=True)
    for ahead in range(1, WIDTH):
        ext = exts[ahead]
        ext[8 : 8 + BLOCK, :] = dpre * cols[:, 1 + ahead : 2 + ahead]
        later = ext[8 + ahead : 8 + ahead + BLOCK, :]
        tap = 3 - ahead
        din = din + cw_ref[tap : tap + 1, :] * later
        cacc_ref[tap : tap + 1, :] += jnp.sum(x * later, axis=0, keepdims=True)
        ext[8 + BLOCK :, :] = ext[8:16, :]
    din_ref[...] = din.astype(BF16)

    @pl.when(turn == pl.num_programs(0) - 1)
    def _():
        halo = halo_ref[...].astype(F32)
        edge = jnp.zeros((8, channels), F32)
        for ahead in range(1, WIDTH):
            ext = exts[ahead]
            ext[0:8, :] = jnp.zeros((8, channels), F32)
            later = ext[ahead : ahead + 8, :]
            tap = 3 - ahead
            edge = edge + cw_ref[tap : tap + 1, :] * later
            cacc_ref[tap : tap + 1, :] += jnp.sum(halo * later, axis=0, keepdims=True)
        edge_ref[...] = edge


def k_dnormed(
    f_ref, dz_ref, din_ref, ddt_ref, own_ref, oth_ref, wg_own, wg_oth, wi_own, wi_oth, ws_own, ws_oth, out_ref, gn_ref
):
    half = own_ref.shape[1]
    inner = dz_ref.shape[1]

    @pl.when(pl.program_id(0) == 0)
    def _():
        gn_ref[...] = jnp.zeros_like(gn_ref)

    dz, dx = dz_ref[...], din_ref[:, :inner]
    small = jnp.concatenate([din_ref[:, inner:], ddt_ref[...]], axis=1)
    own = mm(dz, wg_own[...], NT) + mm(dx, wi_own[...], NT) + mm(small, ws_own[0:half, :], NT)
    oth = mm(dz, wg_oth[...], NT) + mm(dx, wi_oth[...], NT) + mm(small, ws_oth[0:half, :], NT)
    sum_own = jnp.sum(own * own_ref[...].astype(F32), axis=0, keepdims=True)
    sum_oth = jnp.sum(oth * oth_ref[...].astype(F32), axis=0, keepdims=True)

    @pl.when(f_ref[0] == 0)
    def _():
        out_ref[:, :half] = own.astype(BF16)
        out_ref[:, half:] = oth.astype(BF16)
        gn_ref[0:1, :] += sum_own
        gn_ref[1:2, :] += sum_oth

    @pl.when(f_ref[0] != 0)
    def _():
        out_ref[:, :half] = oth.astype(BF16)
        out_ref[:, half:] = own.astype(BF16)
        gn_ref[0:1, :] += sum_oth
        gn_ref[1:2, :] += sum_own


def call(kernel, blocks, ins, outs, scratch=(), backward=False, flops=0, moved=0):
    def turn(i):
        return blocks - 1 - i if backward else i

    def spec(shape, kind):
        if kind == "smem":
            return pl.BlockSpec(memory_space=pltpu.SMEM)
        if kind == "row":
            return pl.BlockSpec((shape[0] // blocks,) + shape[1:], lambda i: (turn(i), 0))
        if kind == "col":
            return pl.BlockSpec((shape[0], shape[1] // blocks), lambda i: (0, turn(i)))
        if kind == "lead":
            return pl.BlockSpec((pl.Squeezed(),) + shape[1:], lambda i: (turn(i), 0, 0))
        return pl.BlockSpec(shape, lambda i: (0,) * len(shape))

    moved = sum(a.size * a.dtype.itemsize for a, _ in ins)
    moved += sum(functools.reduce(lambda p, q: p * q, s, 1) * jnp.dtype(d).itemsize for s, d, _ in outs)
    return pl.pallas_call(
        kernel,
        grid=(blocks,),
        in_specs=[spec(a.shape, kind) for a, kind in ins],
        out_specs=[spec(s, kind) for s, d, kind in outs],
        out_shape=[jax.ShapeDtypeStruct(s, d) for s, d, _ in outs],
        scratch_shapes=list(scratch),
        compiler_params=pltpu.CompilerParams(
            dimension_semantics=("arbitrary",), vmem_limit_bytes=60000 * 1024
        ),
        cost_estimate=pl.CostEstimate(flops=flops, bytes_accessed=moved, transcendentals=0),
    )(*[a for a, _ in ins])


def exchange(a, axis, bit):
    return lax.ppermute(a, axis, [(i, i ^ bit) for i in range(lax.axis_size(axis))])


def swap(a):
    return exchange(a, "fsdp", 1)


def bits(axis):
    n = lax.axis_size(axis)
    return [1 << i for i in range(n.bit_length() - 1)]


def fan(a, axis):
    return [a] + [exchange(a, axis, k) for k in range(1, lax.axis_size(axis))]


def pick_order(parts, index):
    return [lax.select_n(index ^ j, *parts) for j in range(len(parts))]


def in_order(own, other, f, axis):
    return jnp.where(
        f == 0, jnp.concatenate([own, other], axis), jnp.concatenate([other, own], axis)
    )


def sum_over(a, axis):
    for bit in bits(axis):
        a = a + exchange(a, axis, bit)
    return a


def sum_context(a):
    half = a.shape[0] // 2
    order = bits("context")
    done = []
    for part, seq in ((a[:half], order), (a[half:], order[::-1])):
        for i, bit in enumerate(seq):
            part = part.astype(F32) + exchange(part, "context", bit).astype(F32)
            if i < len(seq) - 1:
                part = part.astype(BF16)
        done.append(part)
    return jnp.concatenate(done, axis=0)


def payloads(pay, backward):
    count = lax.axis_size("context")
    if count <= 4:
        sign = -1 if backward else 1
        return [
            lax.ppermute(
                pay, "context", [(i, i + sign * k) for i in range(count) if 0 <= i + sign * k < count]
            )
            for k in range(1, count)
        ]
    place = lax.axis_index("context")
    every = lax.all_gather(pay, "context").astype(F32)
    state = jnp.zeros((STATE, pay.shape[1]), F32)
    for turn in range(count):
        source = count - 1 - turn if backward else turn
        later = every[source, :STATE] + every[source, STATE : STATE + 1] * state
        state = jnp.where(source > place if backward else source < place, later, state)
    return [jnp.concatenate([state, jnp.zeros((PAY - STATE, pay.shape[1]), F32)], axis=0).astype(BF16)]


def on_device(
    hidden, norm_gain, w_gate, w_input, w_bc, w_dt, conv_x, conv_bc, bias_x, bias_bc,
    dt_bias, a_log, skip_d, out_gain, w_out, cotangent, doc_start, valid,
):
    tokens, model = hidden.shape
    inner = w_gate.shape[1]
    heads = w_dt.shape[1]
    half = model // 2
    blocks = tokens // BLOCK
    part = w_bc.shape[1]
    channels = inner + 2 * STATE
    n_tensor = lax.axis_size("tensor")
    n_context = lax.axis_size("context")
    width = inner * n_tensor
    f = lax.axis_index("fsdp")
    t = lax.axis_index("tensor")
    fi = jnp.reshape(f, (1,)).astype(jnp.int32)

    wo_oth = swap(w_out)
    gain_oth = swap(norm_gain)
    wi_oth = swap(w_input)
    cbc = jnp.concatenate([conv_bc, bias_bc[None], jnp.zeros((3, conv_bc.shape[1]), BF16)], axis=0)
    cbc = jnp.pad(cbc, ((0, 0), (0, part - cbc.shape[1])))
    pieces = fan(jnp.concatenate([w_bc, cbc], axis=0), "tensor")
    small_own = jnp.concatenate(
        pick_order(pieces, t) + [jnp.pad(w_dt, ((0, 8), (0, LANES - heads)))], axis=1
    )
    small_oth = swap(small_own)
    mine = conv_x.shape[1]
    own_heads = dt_bias.shape[0]
    third = [jnp.pad(a, (0, mine // 3 - own_heads)) for a in (dt_bias, a_log, skip_d)]
    pack = jnp.concatenate(
        [conv_x, bias_x[None], out_gain[None], jnp.concatenate(third)[None], jnp.zeros((1, mine), BF16)], axis=0
    )
    pack_oth = swap(pack)
    wg_oth = swap(w_gate)
    gain = in_order(norm_gain, gain_oth, f, 0).astype(F32)[None]
    full = in_order(pack, pack_oth, f, 1).astype(F32)
    by_head = full[6].reshape(2, 3, mine // 3)[:, :, :own_heads]
    by_head = jnp.swapaxes(by_head, 0, 1).reshape(3, heads)
    head_rows = jnp.stack([by_head[0], -jnp.exp(by_head[1]), by_head[2]])
    head_rows = jnp.pad(head_rows, ((0, 5), (0, LANES - heads)))
    skip_full = jnp.repeat(by_head[2], HEAD_DIM)
    gate_rows = jnp.concatenate([full[5][None], skip_full[None], jnp.zeros((6, inner), F32)], axis=0)
    few = cbc.shape[1] // 2
    bc_own = small_own[half:, : 2 * STATE].reshape(8, n_tensor, part)[:, :, :few]
    bc_oth = small_oth[half:, : 2 * STATE].reshape(8, n_tensor, part)[:, :, :few]
    taps_bc = in_order(bc_own, bc_oth, f, 2).reshape(8, 2 * STATE).astype(F32)
    taps = jnp.concatenate([full, taps_bc], axis=1)

    starts = doc_start.astype(F32)
    one = jnp.ones((2,), F32)
    m1 = 1.0 - starts
    m2 = m1 * jnp.concatenate([one[:1], m1[:-1]])
    m3 = m2 * jnp.concatenate([one, m1[:-2]])
    rows = jnp.stack([starts, valid.astype(F32), m1, m2, m3] + [jnp.zeros((tokens,), F32)] * 11).astype(BF16)
    keep = jnp.concatenate([jnp.zeros((5,), F32), m2[-1:], m1[-1:], one[:1]])[:, None]

    do, ct_own, ct_oth = call(
        k_do, blocks,
        [(fi, "smem"), (cotangent, "row"), (w_out, "all"), (wo_oth, "all")],
        [((tokens, inner), BF16, "row"), ((tokens, half), BF16, "row"), ((tokens, half), BF16, "row")],
        flops=2 * tokens * model * inner,
    )
    n_own, n_oth, xcat, dt_raw = call(
        k_project, blocks,
        [(fi, "smem"), (hidden, "row"), (gain, "all"), (w_input, "all"), (wi_oth, "all"), (small_own, "all"), (small_oth, "all")],
        [((tokens, half), BF16, "row"), ((tokens, half), BF16, "row"), ((tokens, channels), BF16, "row"), ((tokens, LANES), F32, "row")],
        flops=2 * tokens * model * (channels + LANES),
    )
    edge = (xcat[tokens - 8 :].astype(F32) * keep).astype(BF16)
    halo = lax.ppermute(edge, "context", [(i, i + 1) for i in range(n_context - 1)])
    (z,) = call(
        k_gate_in, blocks,
        [(n_own, "row"), (n_oth, "row"), (w_gate, "all"), (wg_oth, "all")],
        [((tokens, inner), F32, "row")],
        flops=2 * tokens * model * inner,
    )
    act, pre, cs, dt, h_local, d_local, pay = call(
        k_conv, blocks,
        [(rows, "col"), (xcat, "row"), (halo, "all"), (dt_raw, "row"), (head_rows, "all"), (taps, "all")],
        [
            ((tokens, channels), BF16, "row"), ((tokens, channels), BF16, "row"),
            ((tokens, LANES), F32, "row"), ((tokens, LANES), F32, "row"),
            ((blocks, STATE, inner), F32, "lead"), ((blocks, 8, inner), F32, "lead"), ((PAY, inner), BF16, "all"),
        ],
        scratch=[
            pltpu.VMEM((8 + BLOCK, channels), F32), pltpu.VMEM((STATE, inner), F32), pltpu.VMEM((8, inner), F32),
        ],
        flops=2 * tokens * inner * STATE * 8,
    )
    pays = payloads(pay, False)
    n_pay = len(pays)
    (y0,) = call(
        functools.partial(k_heads, heads), blocks,
        [(rows, "col"), (act, "row"), (cs, "row"), (dt, "row"), (gate_rows, "all")],
        [((tokens, inner), F32, "row")],
        flops=16 * tokens * inner * BLOCK,
    )
    y, o_low, stats = call(
        functools.partial(k_gate, n_pay), blocks,
        [
            (rows, "col"), (act, "row"), (cs, "row"), (y0, "row"), (h_local, "lead"), (d_local, "lead"),
            (z, "row"), (do, "row"), (gate_rows, "all"),
        ]
        + [(p, "all") for p in pays],
        [((tokens, inner), F32, "row"), ((tokens, inner), BF16, "row"), ((8, tokens), F32, "col")],
        flops=2 * tokens * inner * STATE * 4,
    )
    others = fan(stats, "tensor")
    (branch,) = call(
        k_branch, blocks,
        [(fi, "smem"), (o_low, "row"), (w_out, "all"), (wo_oth, "all")],
        [((tokens, model), BF16, "row")],
        flops=2 * tokens * model * inner,
    )
    while len(others) > 1:
        others = [others[i] + others[i + 1] for i in range(0, len(others), 2)]
    stats = others[0]
    branch = lax.psum(branch, "tensor")

    dz, o, dxs, dbc, dcs, w, g_local, e_local, gpay, acc = call(
        functools.partial(k_back, heads, width, n_pay), blocks,
        [
            (rows, "col"), (act, "row"), (cs, "row"), (dt, "row"), (y, "row"), (z, "row"), (do, "row"),
            (h_local, "lead"), (d_local, "lead"), (gate_rows, "all"), (stats, "col"),
        ]
        + [(p, "all") for p in pays],
        [
            ((tokens, inner), BF16, "row"), ((tokens, inner), BF16, "row"), ((tokens, inner), F32, "row"),
            ((tokens, 2 * STATE), F32, "row"), ((tokens, LANES), F32, "row"), ((tokens, LANES), F32, "row"),
            ((blocks, STATE, inner), F32, "lead"), ((blocks, 8, inner), F32, "lead"), ((PAY, inner), BF16, "all"),
            ((8, inner), F32, "all"),
        ],
        scratch=[pltpu.VMEM((BLOCK, inner), F32), pltpu.VMEM((STATE, inner), F32), pltpu.VMEM((8, inner), F32)],
        backward=True,
        flops=32 * tokens * inner * BLOCK,
    )
    gpays = payloads(gpay, True)
    gate_oth = mm(n_oth, dz, TN).astype(BF16)
    gate_got = swap(gate_oth)
    gate_own = mm(n_own, dz, TN)
    din, ddt, edge_grad, cacc, hacc = call(
        functools.partial(k_back_state, n_pay, len(gpays)), blocks,
        [
            (rows, "col"), (act, "row"), (pre, "row"), (xcat, "row"), (halo, "all"), (cs, "row"), (dt, "row"),
            (dt_raw, "row"), (dxs, "row"), (dbc, "row"), (dcs, "row"), (w, "row"), (g_local, "lead"), (e_local, "lead"),
            (h_local, "lead"), (d_local, "lead"), (head_rows, "all"), (taps, "all"),
        ]
        + [(p, "all") for p in pays]
        + [(p, "all") for p in gpays],
        [
            ((tokens, channels), BF16, "row"), ((tokens, LANES), BF16, "row"), ((8, channels), F32, "all"),
            ((8, channels), F32, "all"), ((8, LANES), F32, "all"),
        ],
        scratch=[pltpu.VMEM((16 + BLOCK, channels), F32)] * 3,
        backward=True,
        flops=2 * tokens * inner * STATE * 12,
    )
    back = lax.ppermute(edge_grad, "context", [(i, i - 1) for i in range(1, n_context)])
    out_oth = mm(o, ct_oth, TN).astype(BF16)
    out_got = swap(out_oth)
    out_own = mm(o, ct_own, TN)
    tail = (din[tokens - 8 :].astype(F32) + back * keep).astype(BF16)
    din = lax.dynamic_update_slice(din, tail, (tokens - 8, 0))
    dn, gn = call(
        k_dnormed, blocks,
        [
            (fi, "smem"), (dz, "row"), (din, "row"), (ddt, "row"), (n_own, "row"), (n_oth, "row"), (w_gate, "all"),
            (wg_oth, "all"), (w_input, "all"), (wi_oth, "all"), (small_own, "all"), (small_oth, "all"),
        ],
        [((tokens, model), BF16, "row"), ((8, half), F32, "all")],
        flops=2 * tokens * model * (2 * inner + 3 * LANES),
    )
    dn = lax.psum(dn, "tensor")

    in_oth = mm(n_oth, din, TN).astype(BF16)
    step_oth = mm(n_oth, ddt, TN).astype(BF16)
    in_got, step_got = swap(in_oth), swap(step_oth)
    in_own = mm(n_own, din, TN)
    step_own = mm(n_own, ddt, TN)
    grad_gate = sum_context((gate_own + gate_got.astype(F32)).astype(BF16))
    rows_out = sum_context((out_own + out_got.astype(F32)).astype(BF16))
    both = (in_own + in_got.astype(F32)).astype(BF16)
    grad_input = sum_context(both[:, :inner])
    bc = both[:, inner:]
    sent = [
        lax.dynamic_slice(bc, (0, (t ^ k) * part), (half, part)) for k in range(n_tensor)
    ]
    got = [sent[0]] + [exchange(sent[k], "tensor", k) for k in range(1, n_tensor)]
    bc = functools.reduce(lambda p, q: p + q, [g.astype(F32) for g in got])
    step = step_own + step_got.astype(F32)
    few_cols = jnp.concatenate([bc, step[:, : LANES - part]], axis=1).astype(BF16)
    few_cols = sum_context(few_cols)
    grad_bc, grad_step = few_cols[:, :part], few_cols[:, part : part + heads]

    shared = jnp.concatenate([gn, cacc[:, inner:]], axis=1)
    shared = sum_over(shared, "tensor")
    line = jnp.concatenate([hacc[0], hacc[1], jnp.zeros((inner - 2 * LANES,), F32)])
    private = jnp.concatenate([cacc[:5, :inner], acc[:2], line[None]], axis=0)
    little = jnp.concatenate([private, shared], axis=1)
    little = sum_over(sum_over(little, "fsdp"), "context")
    mine_at = f * mine
    conv_rows = lax.dynamic_slice(little, (0, mine_at), (6, mine))
    bc_rows = lax.dynamic_slice(little, (0, inner + half + t * part + f * few), (5, few))
    of_heads = jnp.stack(
        [little[7, :heads], little[7, LANES : LANES + heads], little[6, :inner].reshape(heads, HEAD_DIM).sum(axis=1)]
    )
    of_heads = lax.dynamic_slice(of_heads, (0, f * own_heads), (3, own_heads))
    grad_gain = lax.dynamic_slice(little, (f, inner), (1, half))[0] / norm_gain.astype(F32)

    residual = hidden.astype(F32)
    r2 = lax.rsqrt(stats[0] / width + EPSILON)
    mixed = (residual + branch.astype(F32) * r2[:, None]).astype(BF16)
    r1 = lax.rsqrt(jnp.mean(residual * residual, axis=1, keepdims=True) + EPSILON)
    pulled = dn.astype(F32) * gain
    grad_hidden = (
        cotangent.astype(F32)
        + r1 * pulled
        - residual * (r1**3 / model) * jnp.sum(pulled * residual, axis=1, keepdims=True)
    )
    return (
        mixed, grad_hidden, grad_gain, grad_gate, grad_input, grad_bc, grad_step,
        conv_rows[:4], bc_rows[:4], conv_rows[4], bc_rows[4],
        of_heads[0], of_heads[1], of_heads[2], conv_rows[5], rows_out,
    )


def solution(mesh):
    both = ("fsdp", "context")
    owner = ("tensor", "fsdp")
    params = (
        P("fsdp"), P("fsdp", "tensor"), P("fsdp", "tensor"), P("fsdp", "tensor"), P("fsdp", "tensor"),
        P(None, owner), P(None, owner), P(owner), P(owner), P(owner), P(owner), P(owner), P(owner),
        P("tensor", "fsdp"),
    )
    return jax.shard_map(
        on_device,
        mesh=mesh,
        in_specs=(P(both, None),) + params + (P(both, None), P(both), P(both)),
        out_specs=(P(both, None), P(both, None)) + params,
        check_vma=False,
    )
```
